1024 devices in a mesh: row: 16 (over z, core), col: 64 (over y, x).
Axes of the slice: x: 8, y: 8, z: 8, core: 2. Of those that a mesh axis runs over, the one named last changes fastest.
Arguments:
- matrix: float32 [16384, 16384], P('row', 'col'), may hold values from -2.5 to 2.5
- vectors: float32 [2048, 16384], P('col', 'row'), may hold values from -6 to 6
Outputs:
- reduced: float32 [16384, 16384], P('row', 'col')
- rotated: float32 [2048, 16384], P('col', 'row')
The draws below stay inside these ranges and needn't reach their ends.
All inputs are finite; a program needn't handle non-finite values.
Results may differ from the reference program's by a relative error of at most 0.00012.
Values sent between devices are 32-bit elements; how exact they have to be, the bound alone decides.
No kernel may reach another device: no remote copies, remote signals or barrier semaphores. Data moves between devices by JAX's collectives and lax.ppermute only.
A program may use at most 32 MiB of HBM per device.

```python
import jax
import jax.numpy as jnp
from jax import lax

N = 16384
B = 128
PANELS = 2
NE = 2048


def draw_matrix(key, part):
    normal_key = jax.random.fold_in(jax.random.fold_in(key, 17), 0)
    normal_part = jax.random.normal(normal_key, (N, N), jnp.float32)
    symmetric = (normal_part + normal_part.T) * 0.35355339
    return jnp.clip(symmetric, -2.5, 2.5).astype(jnp.float32)


def steps_of(stream_key, dims, pieces, least, high):
    factor_of, own = 1.0, jax.random.fold_in(stream_key, 6)
    for dim, blocks in pieces:
        draws = jnp.exp(jax.random.uniform(jax.random.fold_in(own, dim), (blocks,), jnp.float32, least / len(pieces), high / len(pieces)))
        factor_of = factor_of * jnp.repeat(draws, dims[dim] // blocks).reshape([-1 if axis == dim else 1 for axis in range(len(dims))])
    return factor_of


def bell_draw(own_key, shape, spread, limit, shards=(), held_as=jnp.bfloat16):
    loudness = steps_of(own_key, shape, shards, -0.22, 0.18) if shards else 1.0
    array = jax.random.normal(own_key, shape, jnp.float32) * spread * loudness
    return jnp.minimum(jnp.maximum(array, -limit), limit).astype(held_as)


def setup_inputs(seed: int = 0) -> dict:
    arg_keys = jax.random.split(jax.random.key(seed), 3)
    return {
        "matrix": draw_matrix(jax.random.fold_in(arg_keys[2], 71), 0),
        "vectors": bell_draw(arg_keys[1], (NE, N), 1.0, 6.0, ((0, 64), (1, 16)), jnp.float32),
    }


precise_mode = lax.Precision.HIGHEST

def dot_plain(left_side, right_side):
    return jnp.dot(left_side.astype(jnp.float32), right_side.astype(jnp.float32), precision=precise_mode, preferred_element_type=jnp.float32)

def dot_inner(left_side, right_side):
    return lax.dot_general(left_side.astype(jnp.float32), right_side.astype(jnp.float32), (((0,), (0,)), ((), ())), precision=precise_mode, preferred_element_type=jnp.float32)

def dot_outer(left_side, right_side):
    return lax.dot_general(left_side.astype(jnp.float32), right_side.astype(jnp.float32), (((1,), (1,)), ((), ())), precision=precise_mode, preferred_element_type=jnp.float32)

def inverse_factor(gram_matrix, identity):
    factor = jnp.linalg.cholesky(gram_matrix)
    return lax.linalg.triangular_solve(factor, identity, left_side=True, lower=True, transpose_a=True)

def solve_leading(leading):
    factor = jnp.linalg.cholesky(dot_outer(leading, leading))
    halfway = lax.linalg.triangular_solve(factor, leading, left_side=True, lower=True)
    return lax.linalg.triangular_solve(factor, halfway, left_side=True, lower=True, transpose_a=True)

def reference(matrix, vectors):
    matrix_order = matrix.shape[0]
    row_index = jnp.arange(matrix_order, dtype=jnp.int32)
    identity = jnp.eye(B, dtype=jnp.float32)
    current = matrix
    stored = []
    for panel_no in range(PANELS):
        first_row = (panel_no + 1) * B
        column_block = current[:, panel_no * B:(panel_no + 1) * B]
        panel_cols = jnp.where((row_index >= first_row)[:, None], column_block, 0.0)
        r_inverse = inverse_factor(dot_inner(panel_cols, panel_cols), identity)
        basis = (row_index[:, None] == first_row + jnp.arange(B, dtype=jnp.int32)[None, :]).astype(jnp.float32)
        reflect = dot_plain(panel_cols, r_inverse) + basis
        t_factor = solve_leading(reflect[first_row:first_row + B])
        product = dot_plain(current, reflect)
        coupling = dot_inner(reflect, product)
        k_factor = dot_plain(dot_inner(t_factor, coupling), t_factor)
        update_w = dot_plain(product, t_factor) - 0.5 * dot_plain(reflect, k_factor)
        current = current - dot_outer(jnp.concatenate([reflect, update_w], 1), jnp.concatenate([update_w, reflect], 1))
        stored.append((reflect, t_factor))
    rotated = vectors
    for reflect, t_factor in reversed(stored):
        weights = dot_plain(rotated, reflect)
        rotated = rotated - dot_outer(dot_outer(weights, t_factor), reflect)
    return (current, rotated)
```

```python
import jax
import jax.numpy as jnp
from jax import lax
from jax.sharding import PartitionSpec as P

B = 128
PANELS = 2
WIDE = PANELS * B


precise_mode = lax.Precision.HIGHEST


def dot_plain(left_side, right_side):
    return jnp.dot(
        left_side, right_side, precision=precise_mode, preferred_element_type=jnp.float32
    )


def dot_inner(left_side, right_side):
    return lax.dot_general(
        left_side,
        right_side,
        (((0,), (0,)), ((), ())),
        precision=precise_mode,
        preferred_element_type=jnp.float32,
    )


def dot_outer(left_side, right_side):
    return lax.dot_general(
        left_side,
        right_side,
        (((1,), (1,)), ((), ())),
        precision=precise_mode,
        preferred_element_type=jnp.float32,
    )


def inverse_factor(gram_matrix, identity):
    factor = jnp.linalg.cholesky(gram_matrix)
    return lax.linalg.triangular_solve(
        factor, identity, left_side=True, lower=True, transpose_a=True
    )


def solve_leading(leading):
    factor = jnp.linalg.cholesky(dot_outer(leading, leading))
    halfway = lax.linalg.triangular_solve(factor, leading, left_side=True, lower=True)
    return lax.linalg.triangular_solve(
        factor, halfway, left_side=True, lower=True, transpose_a=True
    )


def spread(share, axis, count):
    return lax.all_to_all(
        jnp.broadcast_to(share[None], (count, *share.shape)), axis, 0, 0, tiled=True
    )


def make_per_device(row_count, col_count):
    def exchange_rows(stack):
        parts = stack.reshape(row_count, -1, stack.shape[1])
        return lax.all_to_all(parts, "row", 0, 0, tiled=True)

    def per_device(matrix, vectors):
        block_rows, block_cols = matrix.shape
        row_place = lax.axis_index("row")
        col_place = lax.axis_index("col")
        blocks_per_row = block_rows // block_cols
        share_rows = block_cols // row_count
        rows_here = row_place * block_rows + lax.iota(jnp.int32, block_rows)
        cols_here = col_place * block_cols + lax.iota(jnp.int32, block_cols)
        identity = jnp.eye(B, dtype=jnp.float32)
        first_device = row_place == 0
        moves = [
            (
                row * col_count + col,
                (col // blocks_per_row) * col_count + (col % blocks_per_row) * row_count + row,
            )
            for row in range(row_count)
            for col in range(col_count)
        ]

        def to_row_block(share):
            moved = lax.ppermute(share, ("row", "col"), moves)
            return spread(moved, "col", col_count).reshape(block_rows, share.shape[1])

        def on_first(block):
            return jnp.where(first_device, block, 0.0)

        share = exchange_rows(matrix[:WIDE].T)[0]
        lead_rows = to_row_block(share)
        extra = jnp.concatenate([share[:, :B], share[:, B:]], 0)
        current = matrix
        stored = []
        for panel_no in range(PANELS):
            first_row = (panel_no + 1) * B
            wanted = first_row + lax.iota(jnp.int32, B)[None, :]
            part = slice(panel_no * B, (panel_no + 1) * B)
            panel_rows = lead_rows[:, part]
            for reflect, product, top_r, top_y, t_factor, k_factor in stored:
                update = dot_plain(top_y, t_factor) - dot_plain(top_r, k_factor)
                panel_rows = (
                    panel_rows
                    - dot_outer(reflect, update)
                    - dot_plain(product, dot_outer(t_factor, top_r))
                )
            panel_rows = jnp.where((rows_here >= first_row)[:, None], panel_rows, 0.0)
            stack = jnp.concatenate(
                [dot_inner(panel_rows, panel_rows), on_first(panel_rows[first_row : first_row + B])],
                0,
            )
            sums = exchange_rows(stack).sum(0)
            stack_rows = sums.shape[0]
            if panel_no == 0:
                sums = jnp.concatenate([sums, extra], 0)
            gathered = spread(sums, "row", row_count)
            stacked = gathered[:, :stack_rows].reshape(-1, B)
            if panel_no == 0:
                lead_cols = jnp.concatenate(
                    [
                        gathered[:, stack_rows + n * share_rows : stack_rows + (n + 1) * share_rows].reshape(
                            block_cols, B
                        )
                        for n in range(PANELS)
                    ],
                    1,
                )
                panel_cols = lead_cols[:, :B]
            else:
                panel_cols = next_cols
            panel_cols = jnp.where((cols_here >= first_row)[:, None], panel_cols, 0.0)
            r_inverse = inverse_factor(stacked[:B], identity)
            reflect = dot_plain(panel_rows, r_inverse) + (rows_here[:, None] == wanted).astype(
                jnp.float32
            )
            v_cols = dot_plain(panel_cols, r_inverse) + (cols_here[:, None] == wanted).astype(
                jnp.float32
            )
            top_r = dot_plain(stacked[B:], r_inverse) + identity
            t_factor = solve_leading(top_r)
            y_share = exchange_rows(dot_inner(current, reflect)).sum(0)
            product = to_row_block(y_share)
            pieces = [dot_inner(reflect, product), dot_plain(vectors, reflect)]
            if panel_no == 0:
                pieces.append(on_first(product[first_row : first_row + B]))
            else:
                pieces.append(dot_inner(reflect, stored[0][0]))
            rest = -sum(piece.shape[0] for piece in pieces) % (8 * row_count)
            if rest:
                pieces.append(jnp.zeros((rest, B), jnp.float32))
            sums = exchange_rows(jnp.concatenate(pieces, 0)).sum(0)
            gathered = spread(jnp.concatenate([y_share, sums], 0), "row", row_count)
            av_cols = gathered[:, :share_rows].reshape(block_cols, B)
            totals = gathered[:, share_rows:].reshape(-1, B)
            coupling = totals[:B]
            weights = totals[B : B + vectors.shape[0]]
            last = totals[B + vectors.shape[0] : 2 * B + vectors.shape[0]]
            k_factor = dot_plain(dot_inner(t_factor, coupling), t_factor)
            right_first = dot_plain(av_cols, t_factor) - 0.5 * (
                dot_plain(v_cols, k_factor) + dot_outer(v_cols, k_factor)
            )
            right_second = dot_outer(v_cols, t_factor)
            current = current - dot_outer(
                jnp.concatenate([reflect, product], 1),
                jnp.concatenate([right_first, right_second], 1),
            )
            if panel_no == 0:
                top_y, first_weights = last, weights
                stored.append((reflect, product, top_r, top_y, t_factor, 0.5 * (k_factor + k_factor.T)))
                next_cols = (
                    lead_cols[:, B:]
                    - dot_outer(v_cols, dot_plain(top_y, t_factor) - 0.5 * dot_plain(top_r, k_factor + k_factor.T))
                    - dot_plain(av_cols, dot_outer(t_factor, top_r))
                )
        first_reflect, first_t = stored[0][0], stored[0][4]
        second = dot_outer(weights, t_factor)
        first = dot_outer(first_weights - dot_plain(second, last), first_t)
        rotated = vectors - dot_outer(
            jnp.concatenate([second, first], 1), jnp.concatenate([reflect, first_reflect], 1)
        )
        return (current, rotated)

    return per_device


def solution(mesh):
    return jax.shard_map(
        make_per_device(mesh.shape["row"], mesh.shape["col"]),
        mesh=mesh,
        in_specs=(P("row", "col"), P("col", "row")),
        out_specs=(P("row", "col"), P("col", "row")),
        check_vma=False,
    )
```

```python
import jax
import jax.numpy as jnp
from jax import lax
from jax.experimental import pallas as pl
from jax.experimental.pallas import tpu as pltpu
from jax.sharding import PartitionSpec as P

B = 128
PANELS = 2
WIDE = (PANELS + 1) * B
STRIP = 8


precise_mode = lax.Precision.HIGHEST


def dot_over(left_side, right_side, left_dim, right_dim):
    return lax.dot_general(
        left_side,
        right_side,
        (((left_dim,), (right_dim,)), ((), ())),
        precision=precise_mode,
        preferred_element_type=jnp.float32,
    )


def dot_plain(left_side, right_side):
    return dot_over(left_side, right_side, 1, 0)


def dot_inner(left_side, right_side):
    return dot_over(left_side, right_side, 0, 0)


def dot_outer(left_side, right_side):
    return dot_over(left_side, right_side, 1, 1)


def eliminate(work):
    row = lax.broadcasted_iota(jnp.int32, (STRIP, B), 0)
    lane = lax.broadcasted_iota(jnp.int32, (STRIP, B), 1)
    strips = []
    for start in range(0, B, STRIP):
        left = work[start : start + STRIP, :B]
        right = work[start : start + STRIP, B:]
        cols = [
            jnp.broadcast_to(left[:, start + k : start + k + 1], (STRIP, B)) for k in range(STRIP)
        ]
        scale = jnp.ones((STRIP, B), jnp.float32)
        for k in range(STRIP):
            inverse = 1.0 / jnp.broadcast_to(cols[k][k : k + 1], (STRIP, B))
            scale = jnp.where(row == k, inverse, scale)
            if k + 1 < STRIP:
                factor = jnp.where(row > k, cols[k] * inverse, 0.0)
                for n in range(k + 1, STRIP):
                    cols[n] = cols[n] - factor * cols[n][k : k + 1]
                left = left - factor * left[k : k + 1]
                right = right - factor * right[k : k + 1]
        strips.append(right * jnp.sqrt(scale))
        if start + STRIP < B:
            later = jnp.where(lane >= start + STRIP, left, 0.0)
            both = jnp.concatenate([left * scale, right * scale], 1)
            work[...] = work[...] - dot_inner(later, both)
    return jnp.concatenate(strips, 0)


def factor_kernel(gram_ref, top_ref, inverse_ref, leading_ref, t_ref, work):
    row = lax.broadcasted_iota(jnp.int32, (B, B), 0)
    lane = lax.broadcasted_iota(jnp.int32, (B, B), 1)
    identity = (row == lane).astype(jnp.float32)
    work[:, :B] = gram_ref[...]
    work[:, B:] = identity
    lower = eliminate(work)
    inverse_ref[...] = lower.T
    leading = dot_outer(top_ref[...], lower) + identity
    leading_ref[...] = leading
    work[:, :B] = dot_outer(leading, leading)
    work[:, B:] = identity
    lower = eliminate(work)
    t_ref[...] = dot_inner(lower, dot_plain(lower, leading))


def factors(gram_matrix, top_block):
    block = jax.ShapeDtypeStruct((B, B), jnp.float32)
    return pl.pallas_call(
        factor_kernel,
        out_shape=(block, block, block),
        scratch_shapes=[pltpu.VMEM((B, 2 * B), jnp.float32)],
    )(gram_matrix, top_block)


def spread(share, axis, count):
    return lax.all_to_all(
        jnp.broadcast_to(share[None], (count, *share.shape)), axis, 0, 0, tiled=True
    )


def make_per_device(row_count, col_count):
    def split(block):
        return block.reshape(row_count, -1, block.shape[1])

    def exchange(pieces):
        parts = jnp.concatenate([split(piece) for piece in pieces], 1)
        return lax.all_to_all(parts, "row", 0, 0, tiled=True)

    def spread_rows(share):
        return spread(share, "row", row_count)

    def per_device(matrix, vectors):
        block_rows, block_cols = matrix.shape
        row_place = lax.axis_index("row")
        col_place = lax.axis_index("col")
        blocks_per_row = block_rows // block_cols
        size = block_cols // row_count
        part = B // row_count
        rows_here = (row_place * block_rows + lax.iota(jnp.int32, block_rows))[:, None]
        cols_here = (col_place * block_cols + lax.iota(jnp.int32, block_cols))[:, None]
        on_top = row_place == 0
        moves = [
            (
                row * col_count + col,
                (col // blocks_per_row) * col_count + (col % blocks_per_row) * row_count + row,
            )
            for row in range(row_count)
            for col in range(col_count)
        ]

        def moved(share):
            return lax.ppermute(share, ("row", "col"), moves)

        def basis(place, first_row):
            return (place == first_row + lax.iota(jnp.int32, B)[None, :]).astype(jnp.float32)

        def take(gathered, start, stop):
            return gathered[:, start:stop].reshape(-1, gathered.shape[2])

        def product_round(current, p_rows, p_cols, others):
            partial = dot_inner(current, p_rows)
            sums = exchange([partial, dot_inner(p_cols, partial)] + others).sum(0)
            by_col = spread(
                jnp.concatenate([moved(sums[:size]), sums[size : size + part]], 0),
                "col",
                col_count,
            )
            z_rows = take(by_col, 0, size)
            square = spread_rows(by_col[:, size:].sum(0)).reshape(B, B)
            rest = spread_rows(jnp.concatenate([sums[:size], sums[size + part :]], 0))
            pieces, at = [], size
            for other in others:
                step = other.shape[0] // row_count
                pieces.append(take(rest, at, at + step))
                at += step
            return z_rows, take(rest, 0, size), square, pieces

        def coupling_of(square, z_top, r_inverse, corner):
            side = dot_plain(z_top, r_inverse)
            return dot_plain(dot_inner(r_inverse, square), r_inverse) + side + side.T + corner

        share = exchange([matrix[:WIDE].T])[0]
        lead_rows = take(spread(moved(share), "col", col_count), 0, size)
        lead_cols = take(spread_rows(share), 0, size)

        p_rows = jnp.where(rows_here >= B, lead_rows[:, :B], 0.0)
        p_cols = jnp.where(cols_here >= B, lead_cols[:, :B], 0.0)
        head = jnp.where(on_top, lead_rows[B:WIDE], 0.0)
        z_rows, z_cols, square, pieces = product_round(
            matrix,
            p_rows,
            p_cols,
            [
                dot_inner(p_rows, p_rows),
                dot_inner(lead_rows[:, B:], p_rows),
                head[:, :B],
                head[:, B : 2 * B],
                head[B:, 2 * B :],
            ],
        )
        gram_matrix, z_head, head_zero, head_one, corner_two = pieces
        r_inverse, v_one, t_zero = factors(gram_matrix, head_zero[:B])
        v_rows = dot_plain(p_rows, r_inverse) + basis(rows_here, B)
        v_cols = dot_plain(p_cols, r_inverse) + basis(cols_here, B)
        v_head = jnp.concatenate([v_one, dot_plain(head_zero[B:], r_inverse)], 0)
        coupling = coupling_of(square, z_head[:B], r_inverse, head_one[:B])
        k_half = 0.5 * dot_plain(dot_inner(t_zero, coupling), t_zero)
        rt_zero = dot_plain(r_inverse, t_zero)

        def w_of(z_block, one_block, v_block):
            return (
                dot_plain(z_block, rt_zero)
                + dot_plain(one_block, t_zero)
                - dot_plain(v_block, k_half)
            )

        w_rows = w_of(z_rows, lead_rows[:, B : 2 * B], v_rows)
        w_cols = w_of(z_cols, lead_cols[:, B : 2 * B], v_cols)
        w_head = w_of(z_head, head_one, v_head)
        right_cols = jnp.concatenate([w_cols, v_cols], 1)
        right_head = jnp.concatenate([w_head, v_head], 1)
        left_rows = jnp.concatenate([v_rows, w_rows], 1)
        left_cols = jnp.concatenate([v_cols, w_cols], 1)
        current = matrix - dot_outer(left_rows, right_cols)
        next_rows = lead_rows[:, B:] - dot_outer(left_rows, right_head)
        next_cols = lead_cols[:, B:] - dot_outer(left_cols, right_head)
        left_two = jnp.concatenate([v_head[B:], w_head[B:]], 1)
        next_two = jnp.concatenate([head_one[B:], corner_two], 1) - dot_outer(left_two, right_head)

        p_rows = jnp.where(rows_here >= 2 * B, next_rows[:, :B], 0.0)
        p_cols = jnp.where(cols_here >= 2 * B, next_cols[:, :B], 0.0)
        count = vectors.shape[0]
        z_rows, z_cols, square, pieces = product_round(
            current,
            p_rows,
            p_cols,
            [
                dot_inner(p_rows, p_rows),
                dot_inner(next_rows[:, B:], p_rows),
                dot_inner(p_rows, v_rows),
                jnp.concatenate(
                    [
                        dot_plain(vectors, v_rows),
                        dot_plain(vectors, p_rows),
                        jnp.where(on_top, vectors[:, 2 * B : 3 * B], 0.0),
                        jnp.zeros((-3 * count % (8 * row_count), B), jnp.float32),
                    ],
                    0,
                ),
            ],
        )
        gram_matrix, z_two, p_v, sides = pieces
        r_inverse, v_two, t_one = factors(gram_matrix, next_two[:, :B])
        u_rows = dot_plain(p_rows, r_inverse) + basis(rows_here, 2 * B)
        u_cols = dot_plain(p_cols, r_inverse) + basis(cols_here, 2 * B)
        u_v = dot_inner(r_inverse, p_v) + v_head[B:]
        second = dot_outer(
            dot_plain(sides[count : 2 * count], r_inverse) + sides[2 * count : 3 * count], t_one
        )
        first = dot_outer(sides[:count] - dot_plain(second, u_v), t_zero)
        rotated = vectors - dot_outer(
            jnp.concatenate([second, first], 1), jnp.concatenate([u_rows, v_rows], 1)
        )
        coupling = coupling_of(square, z_two, r_inverse, next_two[:, B:])
        k_half = 0.5 * dot_plain(dot_inner(t_one, coupling), t_one)
        rt_one = dot_plain(r_inverse, t_one)
        x_rows = (
            dot_plain(z_rows, rt_one)
            + dot_plain(next_rows[:, B:], t_one)
            - dot_plain(u_rows, k_half)
        )
        x_cols = (
            dot_plain(z_cols, rt_one)
            + dot_plain(next_cols[:, B:], t_one)
            - dot_plain(u_cols, k_half)
        )
        current = current - dot_outer(
            jnp.concatenate([u_rows, x_rows], 1), jnp.concatenate([x_cols, u_cols], 1)
        )
        return (current, rotated)

    return per_device


def solution(mesh):
    return jax.shard_map(
        make_per_device(mesh.shape["row"], mesh.shape["col"]),
        mesh=mesh,
        in_specs=(P("row", "col"), P("col", "row")),
        out_specs=(P("row", "col"), P("col", "row")),
        check_vma=False,
    )
```

```python
import jax
import jax.numpy as jnp
from jax import lax
from jax.experimental import pallas as pl
from jax.experimental.pallas import tpu as pltpu
from jax.sharding import PartitionSpec as P

B = 128
PANELS = 2
WIDE = (PANELS + 1) * B
STRIP = 8


precise_mode = lax.Precision.HIGHEST


def dot_over(left_side, right_side, left_dim, right_dim):
    return lax.dot_general(
        left_side,
        right_side,
        (((left_dim,), (right_dim,)), ((), ())),
        precision=precise_mode,
        preferred_element_type=jnp.float32,
    )


def dot_plain(left_side, right_side):
    return dot_over(left_side, right_side, 1, 0)


def large_dot(left_side, right_side, left_dim, right_dim):
    return lax.dot_general(
        left_side,
        right_side,
        (((left_dim,), (right_dim,)), ((), ())),
        precision=lax.Precision.HIGH,
        preferred_element_type=jnp.float32,
    )


def dot_inner(left_side, right_side):
    return dot_over(left_side, right_side, 0, 0)


def dot_outer(left_side, right_side):
    return dot_over(left_side, right_side, 1, 1)


def eliminate(work):
    row = lax.broadcasted_iota(jnp.int32, (STRIP, B), 0)
    lane = lax.broadcasted_iota(jnp.int32, (STRIP, B), 1)
    strips = []
    for start in range(0, B, STRIP):
        left = work[start : start + STRIP, :B]
        right = work[start : start + STRIP, B:]
        cols = [
            jnp.broadcast_to(left[:, start + k : start + k + 1], (STRIP, B)) for k in range(STRIP)
        ]
        scale = jnp.ones((STRIP, B), jnp.float32)
        for k in range(STRIP):
            inverse = 1.0 / jnp.broadcast_to(cols[k][k : k + 1], (STRIP, B))
            scale = jnp.where(row == k, inverse, scale)
            if k + 1 < STRIP:
                factor = jnp.where(row > k, cols[k] * inverse, 0.0)
                for n in range(k + 1, STRIP):
                    cols[n] = cols[n] - factor * cols[n][k : k + 1]
                left = left - factor * left[k : k + 1]
                right = right - factor * right[k : k + 1]
        strips.append(right * jnp.sqrt(scale))
        if start + STRIP < B:
            later = jnp.where(lane >= start + STRIP, left, 0.0)
            both = jnp.concatenate([left * scale, right * scale], 1)
            work[...] = work[...] - dot_inner(later, both)
    return jnp.concatenate(strips, 0)


def factor_kernel(gram_ref, top_ref, inverse_ref, leading_ref, t_ref, work):
    row = lax.broadcasted_iota(jnp.int32, (B, B), 0)
    lane = lax.broadcasted_iota(jnp.int32, (B, B), 1)
    identity = (row == lane).astype(jnp.float32)
    work[:, :B] = gram_ref[...]
    work[:, B:] = identity

    def turn(number, carry):
        lower = eliminate(work)

        @pl.when(number == 0)
        def _():
            inverse_ref[...] = lower.T
            leading = dot_outer(top_ref[...], lower) + identity
            leading_ref[...] = leading
            work[:, :B] = dot_outer(leading, leading)
            work[:, B:] = identity

        @pl.when(number == 1)
        def _():
            t_ref[...] = dot_inner(lower, dot_plain(lower, leading_ref[...]))

        return carry

    lax.fori_loop(0, 2, turn, 0)


def factors(gram_matrix, top_block):
    block = jax.ShapeDtypeStruct((B, B), jnp.float32)
    return pl.pallas_call(
        factor_kernel,
        out_shape=(block, block, block),
        scratch_shapes=[pltpu.VMEM((B, 2 * B), jnp.float32)],
    )(gram_matrix, top_block)


def spread(share, axis, count):
    return lax.all_to_all(
        jnp.broadcast_to(share[None], (count, *share.shape)), axis, 0, 0, tiled=True
    )


def make_per_device(row_count, col_count):
    def split(block):
        return block.reshape(row_count, -1, block.shape[1])

    def exchange(pieces):
        parts = jnp.concatenate([split(piece) for piece in pieces], 1)
        return lax.all_to_all(parts, "row", 0, 0, tiled=True)

    def spread_rows(share):
        return spread(share, "row", row_count)

    def per_device(matrix, vectors):
        block_rows, block_cols = matrix.shape
        row_place = lax.axis_index("row")
        col_place = lax.axis_index("col")
        blocks_per_row = block_rows // block_cols
        size = block_cols // row_count
        part = B // row_count
        rows_here = (row_place * block_rows + lax.iota(jnp.int32, block_rows))[:, None]
        cols_here = (col_place * block_cols + lax.iota(jnp.int32, block_cols))[:, None]
        on_top = row_place == 0
        moves = [
            (
                row * col_count + col,
                (col // blocks_per_row) * col_count + (col % blocks_per_row) * row_count + row,
            )
            for row in range(row_count)
            for col in range(col_count)
        ]

        def moved(share):
            return lax.ppermute(share, ("row", "col"), moves)

        def basis(place, first_row):
            return (place == first_row + lax.iota(jnp.int32, B)[None, :]).astype(jnp.float32)

        def take(gathered, start, stop):
            return gathered[:, start:stop].reshape(-1, gathered.shape[2])

        def product_round(current, p_rows, p_cols, others):
            partial = large_dot(current, p_rows, 0, 0)
            sums = exchange([partial, large_dot(p_cols, partial, 0, 0)] + others).sum(0)
            by_col = spread(
                jnp.concatenate([moved(sums[:size]), sums[size : size + part]], 0),
                "col",
                col_count,
            )
            z_rows = take(by_col, 0, size)
            square = spread_rows(by_col[:, size:].sum(0)).reshape(B, B)
            rest = spread_rows(jnp.concatenate([sums[:size], sums[size + part :]], 0))
            pieces, at = [], size
            for other in others:
                step = other.shape[0] // row_count
                pieces.append(take(rest, at, at + step))
                at += step
            return z_rows, take(rest, 0, size), square, pieces

        def coupling_of(square, z_top, r_inverse, corner):
            side = dot_plain(z_top, r_inverse)
            return dot_plain(dot_inner(r_inverse, square), r_inverse) + side + side.T + corner

        share = exchange([matrix[:WIDE].T])[0]
        row_share, lead_cols = lax.optimization_barrier((moved(share), spread_rows(share)))
        lead_rows = take(spread(row_share, "col", col_count), 0, size)
        lead_cols = take(lead_cols, 0, size)

        p_rows = jnp.where(rows_here >= B, lead_rows[:, :B], 0.0)
        p_cols = jnp.where(cols_here >= B, lead_cols[:, :B], 0.0)
        head = jnp.where(on_top, lead_rows[B:WIDE], 0.0)
        z_rows, z_cols, square, pieces = product_round(
            matrix,
            p_rows,
            p_cols,
            [
                dot_inner(p_rows, p_rows),
                large_dot(lead_rows[:, B:], p_rows, 0, 0),
                head[:, :B],
                head[:, B : 2 * B],
                head[B:, 2 * B :],
            ],
        )
        gram_matrix, z_head, head_zero, head_one, corner_two = pieces
        r_inverse, v_one, t_zero = factors(gram_matrix, head_zero[:B])
        v_rows = large_dot(p_rows, r_inverse, 1, 0) + basis(rows_here, B)
        v_cols = large_dot(p_cols, r_inverse, 1, 0) + basis(cols_here, B)
        v_head = jnp.concatenate([v_one, dot_plain(head_zero[B:], r_inverse)], 0)
        coupling = coupling_of(square, z_head[:B], r_inverse, head_one[:B])
        k_half = 0.5 * dot_plain(dot_inner(t_zero, coupling), t_zero)
        rt_zero = dot_plain(r_inverse, t_zero)

        def w_of(z_block, one_block, v_block):
            return (
                large_dot(z_block, rt_zero, 1, 0)
                + large_dot(one_block, t_zero, 1, 0)
                - large_dot(v_block, k_half, 1, 0)
            )

        w_rows = w_of(z_rows, lead_rows[:, B : 2 * B], v_rows)
        w_cols = w_of(z_cols, lead_cols[:, B : 2 * B], v_cols)
        w_head = w_of(z_head, head_one, v_head)
        right_cols = jnp.concatenate([w_cols, v_cols], 1)
        right_head = jnp.concatenate([w_head, v_head], 1)
        left_rows = jnp.concatenate([v_rows, w_rows], 1)
        left_cols = jnp.concatenate([v_cols, w_cols], 1)
        current = matrix - large_dot(left_rows, right_cols, 1, 1)
        next_rows = lead_rows[:, B:] - large_dot(left_rows, right_head, 1, 1)
        next_cols = lead_cols[:, B:] - large_dot(left_cols, right_head, 1, 1)
        left_two = jnp.concatenate([v_head[B:], w_head[B:]], 1)
        next_two = jnp.concatenate([head_one[B:], corner_two], 1) - dot_outer(left_two, right_head)

        p_rows = jnp.where(rows_here >= 2 * B, next_rows[:, :B], 0.0)
        p_cols = jnp.where(cols_here >= 2 * B, next_cols[:, :B], 0.0)
        count = vectors.shape[0]
        z_rows, z_cols, square, pieces = product_round(
            current,
            p_rows,
            p_cols,
            [
                dot_inner(p_rows, p_rows),
                large_dot(next_rows[:, B:], p_rows, 0, 0),
                large_dot(p_rows, v_rows, 0, 0),
                jnp.concatenate(
                    [
                        large_dot(vectors, v_rows, 1, 0),
                        large_dot(vectors, p_rows, 1, 0),
                        jnp.where(on_top, vectors[:, 2 * B : 3 * B], 0.0),
                        jnp.zeros((-3 * count % (8 * row_count), B), jnp.float32),
                    ],
                    0,
                ),
            ],
        )
        gram_matrix, z_two, p_v, sides = pieces
        r_inverse, v_two, t_one = factors(gram_matrix, next_two[:, :B])
        u_rows = large_dot(p_rows, r_inverse, 1, 0) + basis(rows_here, 2 * B)
        u_cols = large_dot(p_cols, r_inverse, 1, 0) + basis(cols_here, 2 * B)
        u_v = dot_inner(r_inverse, p_v) + v_head[B:]
        second = dot_outer(
            dot_plain(sides[count : 2 * count], r_inverse) + sides[2 * count : 3 * count], t_one
        )
        first = dot_outer(sides[:count] - dot_plain(second, u_v), t_zero)
        rotated = vectors - large_dot(
            jnp.concatenate([second, first], 1), jnp.concatenate([u_rows, v_rows], 1), 1, 1
        )
        coupling = coupling_of(square, z_two, r_inverse, next_two[:, B:])
        k_half = 0.5 * dot_plain(dot_inner(t_one, coupling), t_one)
        rt_one = dot_plain(r_inverse, t_one)
        x_rows = (
            large_dot(z_rows, rt_one, 1, 0)
            + large_dot(next_rows[:, B:], t_one, 1, 0)
            - large_dot(u_rows, k_half, 1, 0)
        )
        x_cols = (
            large_dot(z_cols, rt_one, 1, 0)
            + large_dot(next_cols[:, B:], t_one, 1, 0)
            - large_dot(u_cols, k_half, 1, 0)
        )
        current = current - large_dot(
            jnp.concatenate([u_rows, x_rows], 1), jnp.concatenate([x_cols, u_cols], 1), 1, 1
        )
        return (current, rotated)

    return per_device


def solution(mesh):
    return jax.shard_map(
        make_per_device(mesh.shape["row"], mesh.shape["col"]),
        mesh=mesh,
        in_specs=(P("row", "col"), P("col", "row")),
        out_specs=(P("row", "col"), P("col", "row")),
        check_vma=False,
    )
```
